256 devices in a mesh: seq: 64 (over z_lo, y, x, core), ch: 4 (over z_hi).
Axes of the slice: x: 4, y: 4, z: 8 (z_hi: 4, z_lo: 2; z = z_hi * 2 + z_lo), core: 2. Of those that a mesh axis runs over, the one named last changes fastest.
Arguments:
- inputs: bfloat16 [256, 32768], P('ch', 'seq'), may hold values from -6 to 6
- w_value: bfloat16 [256, 256], P(None, 'ch'), may hold values from -0.375 to 0.375
- w_gate: bfloat16 [256, 256], P(None, 'ch'), may hold values from -0.375 to 0.375
- w_out: bfloat16 [256, 256], P('ch'), may hold values from -0.375 to 0.375
- filter_taps: float32 [256, 32768], P('ch', 'seq'), may hold values from -6 to 6
- grad_out: bfloat16 [256, 32768], P('ch', 'seq'), may hold values from -6 to 6
Outputs:
- d_inputs: bfloat16 [256, 32768], P('ch', 'seq')
- d_w_value: float32 [256, 256], P(None, 'ch')
- d_w_gate: float32 [256, 256], P(None, 'ch')
- d_w_out: float32 [256, 256], P('ch')
- d_filter: float32 [256, 32768], P('ch', 'seq')
The draws below stay inside these ranges and needn't reach their ends.
All inputs are finite; a program needn't handle non-finite values.
Results may differ from the reference program's by a relative error of at most 0.015.
Values may be sent and summed in bfloat16 or wider, within the bound.
No kernel may reach another device: no remote copies, remote signals or barrier semaphores. Data moves between devices by JAX's collectives and lax.ppermute only.
A program may use at most 64 MiB of HBM per device.

```python
import math
import jax
import jax.numpy as jnp

D = 256
TOKENS = 32768


def draw_filter_taps(key, part):
    inner_key = jax.random.fold_in(key, 17)
    key_rate, key_jitter = jax.random.split(inner_key)
    upper_log = math.log(3.0 * TOKENS)
    lower_log = math.log(40.0)
    jitter = jax.random.truncated_normal(key_jitter, -6.0, 6.0, (D, TOKENS), jnp.float32)
    timescale = jnp.exp(lower_log + (upper_log - lower_log) * jax.random.uniform(key_rate, (D, 1), jnp.float32))
    decay_rate = 1.0 / timescale
    positions = jnp.arange(TOKENS, dtype=jnp.float32)[None, :]
    normalizer = jnp.sqrt((1.0 - jnp.exp(-2.0 * decay_rate)) / (1.0 - jnp.exp(-2.0 * TOKENS * decay_rate)))
    return (jitter * jnp.exp(-decay_rate * positions) * normalizer).astype(jnp.float32)


def steps_of(stream_key, shape, cuts, low, high):
    gain = 1.0
    for axis_at, parts in cuts:
        steps = jax.random.uniform(jax.random.fold_in(jax.random.fold_in(stream_key, 6), axis_at), (parts,), jnp.float32, low / len(cuts), high / len(cuts))
        gain = gain * jnp.repeat(jnp.exp(steps), shape[axis_at] // parts).reshape((-1,) + (1,) * (len(shape) - 1 - axis_at))
    return gain


def normal_values(stream_key, shape, width, bound, pieces=(), kind=jnp.bfloat16):
    result = width * jax.random.normal(stream_key, shape, jnp.float32)
    if pieces:
        result = result * steps_of(stream_key, shape, pieces, -0.22, 0.18)
    return jnp.clip(result, -bound, bound).astype(kind)


def setup_inputs(seed: int = 0) -> dict:
    seeds = jax.random.split(jax.random.key(seed), 7)
    return {
        "inputs": normal_values(seeds[0], (D, TOKENS), 1.0, 6.0, ((0, 4), (1, 64))),
        "w_value": normal_values(seeds[1], (D, D), D ** -0.5, 0.375, ((1, 4),)),
        "w_gate": normal_values(seeds[2], (D, D), D ** -0.5, 0.375, ((1, 4),)),
        "w_out": normal_values(seeds[3], (D, D), D ** -0.5, 0.375, ((0, 4),)),
        "filter_taps": draw_filter_taps(jax.random.fold_in(seeds[6], 71), 0),
        "grad_out": normal_values(seeds[5], (D, TOKENS), 1.0, 6.0, ((0, 4), (1, 64))),
    }


def reference(inputs, w_value, w_gate, w_out, filter_taps, grad_out):
    padded_len = 2 * TOKENS
    value_proj = jnp.dot(w_value.T, inputs, preferred_element_type=jnp.float32)
    gate_proj = jnp.dot(w_gate.T, inputs, preferred_element_type=jnp.float32)
    spec_filter = jnp.fft.rfft(filter_taps, n=padded_len, axis=1)
    spec_value = jnp.fft.rfft(value_proj, n=padded_len, axis=1)
    mixed_seq = jnp.fft.irfft(spec_filter * spec_value, n=padded_len, axis=1)[:, :TOKENS]
    gated_out = (gate_proj * mixed_seq).astype(jnp.bfloat16)
    d_gated = jnp.dot(w_out, grad_out, preferred_element_type=jnp.float32)
    d_gate = (d_gated * mixed_seq).astype(jnp.bfloat16)
    d_mixed = d_gated * gate_proj
    spec_grad = jnp.fft.rfft(d_mixed, n=padded_len, axis=1)
    d_value = jnp.fft.irfft(jnp.conj(spec_filter) * spec_grad, n=padded_len, axis=1)[:, :TOKENS]
    d_value = d_value.astype(jnp.bfloat16)
    filter_raw = jnp.fft.irfft(jnp.conj(spec_value) * spec_grad, n=padded_len, axis=1)[:, :TOKENS]
    grad_scale = TOKENS ** -0.5
    d_inputs = jnp.dot(w_value, d_value, preferred_element_type=jnp.float32)
    d_inputs = d_inputs + jnp.dot(w_gate, d_gate, preferred_element_type=jnp.float32)
    d_inputs = d_inputs.astype(jnp.bfloat16)
    d_w_value = jnp.dot(inputs, d_value.T, preferred_element_type=jnp.float32) * grad_scale
    d_w_gate = jnp.dot(inputs, d_gate.T, preferred_element_type=jnp.float32) * grad_scale
    d_w_out = jnp.dot(gated_out, grad_out.T, preferred_element_type=jnp.float32) * grad_scale
    d_filter = filter_raw.astype(jnp.float32) * grad_scale
    return d_inputs, d_w_value, d_w_gate, d_w_out, d_filter
```

```python
import math

import jax
import jax.numpy as jnp
import ml_dtypes
import numpy as np
from jax import lax
from jax.experimental import pallas as pl
from jax.experimental.pallas import tpu as pltpu
from jax.sharding import PartitionSpec as P

F32 = jnp.float32
BF16 = jnp.bfloat16
LANES = 128
GROUP = 16


def halves(table):
    high = table.astype(ml_dtypes.bfloat16)
    low = (table - high.astype(np.float64)).astype(ml_dtypes.bfloat16)
    return high, low


def transform_tables(tokens):
    rows = tokens // LANES
    length = 2 * tokens
    per_sender = rows // 64
    order = np.arange(rows).reshape(64 // GROUP, GROUP, per_sender)
    order = order.transpose(0, 2, 1).reshape(-1)
    k1 = np.arange(rows) + 0.5
    theta = 2.0 * np.pi * ((k1[:, None] * order[None, :]) % (2 * rows)) / (2 * rows)
    outer = np.concatenate([np.cos(theta), -np.sin(theta)], axis=0)
    q = np.arange(LANES)
    phi = 2.0 * np.pi * ((q[:, None] * q[None, :]) % LANES) / LANES
    c, s = np.cos(phi), np.sin(phi)
    inner = np.block([[c, -s], [s, c]])
    twist = 2.0 * np.pi * k1[:, None] * q[None, :] / length
    twiddle = np.stack([np.cos(twist), -np.sin(twist)]).astype(np.float32)
    scale = 2.0 / length
    return halves(outer) + halves(inner) + halves(inner.T) + halves(outer.T * scale) + (twiddle,)


def exchange_table():
    table = np.zeros((GROUP * GROUP, GROUP * GROUP), np.float32)
    for a in range(GROUP):
        for b in range(GROUP):
            table[a * GROUP + b, b * GROUP + a] = 1.0
    return table.astype(ml_dtypes.bfloat16)


def dot(left, right, dims=((1,), (0,))):
    return lax.dot_general(left, right, (dims, ((), ())), preferred_element_type=F32)


def split_up(value):
    high = value.astype(BF16)
    return high, (value - high.astype(F32)).astype(BF16)


def dot3_left(table_high, table_low, value):
    high, low = split_up(value)
    return dot(table_high, high) + (dot(table_high, low) + dot(table_low, high))


def dot3_right(value, table_high, table_low):
    high, low = split_up(value)
    return dot(high, table_high) + (dot(low, table_high) + dot(high, table_low))


def write_messages(out_ref, swap, parts):
    for g in range(64 // GROUP):
        rows = jnp.concatenate([x[g * GROUP : (g + 1) * GROUP] for x in parts], axis=0)
        out_ref[g * GROUP * GROUP : (g + 1) * GROUP * GROUP, :] = dot(swap, rows).astype(BF16)


def read_messages(in_ref, swap):
    size = GROUP * GROUP
    return [
        dot(swap, in_ref[g * size : (g + 1) * size, :]).astype(BF16) for g in range(64 // GROUP)
    ]


def lane_blocks(value):
    return [value[:, u * LANES : (u + 1) * LANES] for u in range(value.shape[1] // LANES)]


def project_kernel(
    ch_ref, own_ref, got1_ref, got3_ref, got2_ref, wv_ref, wg_ref, wo_ref, taps_ref, swap_ref,
    msg_ref, gate_ref, dgated_ref, in_ref, grad_ref,
):
    ch = ch_ref[0]
    for shift, ref in ((0, own_ref), (1, got1_ref), (3, got3_ref), (2, got2_ref)):
        at = pl.multiple_of(lax.rem(ch + (4 - shift), 4) * 64, 64)
        in_ref[pl.ds(at, 64), :] = ref[:64, :]
        grad_ref[pl.ds(at, 64), :] = ref[64:, :]
    full_in = in_ref[...]
    value = dot(wv_ref[...], full_in).astype(BF16)
    gate = dot(wg_ref[...], full_in)
    d_gated = dot(wo_ref[...], grad_ref[...])
    gate_ref[...] = gate
    dgated_ref[...] = d_gated
    d_mixed = (d_gated * gate).astype(BF16)
    tap_high, tap_low = split_up(taps_ref[...])
    parts = []
    for x in (value, d_mixed, tap_high, tap_low):
        parts += lane_blocks(x)
    write_messages(msg_ref, swap_ref[...], parts)


def convolve_kernel(
    got_ref, swap_ref, oh_ref, ol_ref, ih_ref, il_ref, jh_ref, jl_ref, ph_ref, pl_ref, tw_ref,
    out_ref,
):
    swap = swap_ref[...]
    groups = read_messages(got_ref, swap)

    def signal(k):
        return jnp.concatenate([x[k * 64 : (k + 1) * 64] for x in groups], axis=0)

    data = jnp.concatenate([signal(k) for k in range(4)], axis=1)
    first = dot(oh_ref[...], data) + dot(ol_ref[...], data)
    half = first.shape[0] // 2
    tw_re, tw_im = tw_ref[0], tw_ref[1]

    def column(k):
        return first[:, k * LANES : (k + 1) * LANES]

    spectra = []
    for a in (column(0), column(1), column(2) + column(3)):
        re, im = a[:half], a[half:]
        z = jnp.concatenate([re * tw_re - im * tw_im, re * tw_im + im * tw_re], axis=1)
        x = dot3_right(z, ih_ref[...], il_ref[...])
        spectra.append((x[:, :LANES], x[:, LANES:]))
    (v_re, v_im), (d_re, d_im), (h_re, h_im) = spectra
    products = (
        (h_re * v_re - h_im * v_im, h_re * v_im + h_im * v_re),
        (h_re * d_re + h_im * d_im, h_re * d_im - h_im * d_re),
        (v_re * d_re + v_im * d_im, v_re * d_im - v_im * d_re),
    )
    back = []
    for re, im in products:
        y = dot3_right(jnp.concatenate([re, im], axis=1), jh_ref[...], jl_ref[...])
        re, im = y[:, :LANES], y[:, LANES:]
        b = jnp.concatenate([re * tw_re + im * tw_im, im * tw_re - re * tw_im], axis=0)
        back.append(dot3_left(ph_ref[...], pl_ref[...], b))
    mixed, d_value, d_filter = back
    filter_high, filter_low = split_up(d_filter)
    size = GROUP * GROUP
    for g in range(64 // GROUP):
        rows = jnp.concatenate(
            [
                x[g * 64 : (g + 1) * 64]
                for x in (mixed.astype(BF16), d_value.astype(BF16), filter_high, filter_low)
            ],
            axis=0,
        )
        out_ref[g * size : (g + 1) * size, :] = dot(swap, rows).astype(BF16)


def gradient_kernel(
    ch_ref, got_ref, swap_ref, gate_ref, dgated_ref, in_ref, grad_ref, wv_ref, wg_ref,
    sums_ref, own_ref, send1_ref, send3_ref, send2_ref, filt_ref, part_ref, *, scale
):
    groups = read_messages(got_ref, swap_ref[...])

    def signal(k):
        cols = []
        for u in range(4):
            at = (k * 4 + u) * GROUP
            cols.append(jnp.concatenate([x[at : at + GROUP] for x in groups], axis=0))
        return jnp.concatenate(cols, axis=1)

    mixed = signal(0).astype(F32)
    d_value = signal(1)
    filt_ref[...] = (signal(2).astype(F32) + signal(3).astype(F32)) * scale
    gated_out = (gate_ref[...] * mixed).astype(BF16)
    d_gate = (dgated_ref[...] * mixed).astype(BF16)
    both = jnp.concatenate([d_value, d_gate], axis=0)
    weights = jnp.concatenate([wv_ref[...], wg_ref[...]], axis=0)
    part_ref[...] = dot(weights, both, ((0,), (0,)))
    ch = ch_ref[0]

    def block(shift):
        at = pl.multiple_of(lax.rem(ch + shift, 4) * 64, 64)
        return part_ref[pl.ds(at, 64), :]

    own_ref[...] = block(0)
    send1_ref[...] = block(1).astype(BF16)
    send3_ref[...] = block(3).astype(BF16)
    send2_ref[...] = block(2).astype(BF16)
    term = dot(both, in_ref[...], ((1,), (1,)))
    out_term = dot(gated_out, grad_ref[...], ((1,), (1,)))
    pieces = lane_blocks(term[:64]) + lane_blocks(term[64:]) + lane_blocks(out_term)
    pieces += [jnp.zeros_like(pieces[0])] * 2
    for r, piece in enumerate(pieces):
        sums_ref[pl.ds(r, 64, stride=8), :] = piece


def total_kernel(got_ref, out_ref, *, scale):
    total = got_ref[...].reshape(64, 8, LANES).sum(axis=0) * scale
    out_ref[...] = jnp.broadcast_to(total[None], (64, 8, LANES)).reshape(512, LANES)


def settle_kernel(got_ref, dwv_ref, dwg_ref, dwo_ref):
    for k, ref in enumerate((dwv_ref, dwg_ref, dwo_ref)):
        ref[...] = jnp.concatenate(
            [got_ref[pl.ds(2 * k + j, 64, stride=8), :] for j in range(2)], axis=1
        )


def shaped(shape, dtype):
    return jax.ShapeDtypeStruct(shape, dtype)


VMEM = pl.BlockSpec(memory_space=pltpu.VMEM)
SMEM = pl.BlockSpec(memory_space=pltpu.SMEM)


def exchanged(rows, axis):
    count = lax.axis_size(axis)
    parts = rows.reshape(count, rows.shape[0] // count, rows.shape[1])
    return lax.all_to_all(parts, axis, 0, 0, tiled=True).reshape(rows.shape)


def shifted(value, shift):
    return lax.ppermute(value, "ch", [(i, (i + shift) % 4) for i in range(4)])


def on_device(inputs, w_value, w_gate, w_out, filter_taps, grad_out):
    tokens = filter_taps.shape[1] * lax.axis_size("seq")
    scale = 1.0 / math.sqrt(tokens)
    tables = [jnp.asarray(t) for t in transform_tables(tokens)]
    swap = jnp.asarray(exchange_table())
    ch = lax.axis_index("ch").astype(jnp.int32).reshape(1)
    wv, wg = w_value.T, w_gate.T

    own = jnp.concatenate([inputs, grad_out], axis=0)
    got = [shifted(own, s) for s in (1, 3, 2)]
    msg, gate, d_gated, full_in, full_grad = pl.pallas_call(
        project_kernel,
        out_shape=(
            shaped((1024, LANES), BF16),
            shaped((64, 512), F32),
            shaped((64, 512), F32),
            shaped((256, 512), BF16),
            shaped((256, 512), BF16),
        ),
        in_specs=[SMEM] + [VMEM] * 9,
        out_specs=[VMEM] * 5,
        name="project",
    )(ch, own, *got, wv, wg, w_out, filter_taps, swap)
    back = pl.pallas_call(
        convolve_kernel,
        out_shape=shaped((1024, LANES), BF16),
        in_specs=[VMEM] * 11,
        out_specs=VMEM,
        name="convolve",
    )(exchanged(msg, "seq"), swap, *tables)
    sums, mine, send1, send3, send2, d_filter = pl.pallas_call(
        lambda *refs: gradient_kernel(*refs, scale=scale),
        out_shape=(
            shaped((512, LANES), F32),
            shaped((64, 512), F32),
            shaped((64, 512), BF16),
            shaped((64, 512), BF16),
            shaped((64, 512), BF16),
            shaped((64, 512), F32),
        ),
        in_specs=[SMEM] + [VMEM] * 8,
        out_specs=[VMEM] * 6,
        scratch_shapes=[pltpu.VMEM((256, 512), F32)],
        name="gradients",
    )(ch, exchanged(back, "seq"), swap, gate, d_gated, full_in, full_grad, wv, wg)
    came = [shifted(x, s) for x, s in ((send1, 1), (send3, 3), (send2, 2))]
    d_inputs = mine
    for x in came:
        d_inputs = d_inputs + x.astype(F32)
    d_inputs = d_inputs.astype(BF16)
    total = pl.pallas_call(
        lambda *refs: total_kernel(*refs, scale=scale),
        out_shape=shaped((512, LANES), F32),
        in_specs=[VMEM],
        out_specs=VMEM,
        name="total",
    )(exchanged(sums, "seq"))
    dwv, dwg, dwo = pl.pallas_call(
        settle_kernel,
        out_shape=(shaped((64, 256), F32),) * 3,
        in_specs=[VMEM],
        out_specs=[VMEM] * 3,
        name="settle",
    )(exchanged(total, "seq"))
    return d_inputs, dwv.T, dwg.T, dwo, d_filter


def solution(mesh):
    placed = (
        P("ch", "seq"),
        P(None, "ch"),
        P(None, "ch"),
        P("ch", None),
        P("ch", "seq"),
        P("ch", "seq"),
    )
    return jax.shard_map(
        on_device,
        mesh=mesh,
        in_specs=placed,
        out_specs=(P("ch", "seq"), P(None, "ch"), P(None, "ch"), P("ch", None), P("ch", "seq")),
        check_vma=False,
    )
```

```python
import math

import jax
import jax.numpy as jnp
import ml_dtypes
import numpy as np
from jax import lax
from jax.experimental import pallas as pl
from jax.experimental.pallas import tpu as pltpu
from jax.sharding import PartitionSpec as P


F32 = jnp.float32
BF16 = jnp.bfloat16
LANES = 128
GROUP = 16


def halves(table):
    high = table.astype(ml_dtypes.bfloat16)
    low = (table - high.astype(np.float64)).astype(ml_dtypes.bfloat16)
    return high, low


def transform_tables(tokens):
    rows = tokens // LANES
    length = 2 * tokens
    per_sender = rows // 64
    order = np.arange(rows).reshape(64 // GROUP, GROUP, per_sender)
    order = order.transpose(0, 2, 1).reshape(-1)
    k1 = np.arange(rows) + 0.5
    theta = 2.0 * np.pi * ((k1[:, None] * order[None, :]) % (2 * rows)) / (2 * rows)
    outer = np.concatenate([np.cos(theta), -np.sin(theta)], axis=0)
    q = np.arange(LANES)
    phi = 2.0 * np.pi * ((q[:, None] * q[None, :]) % LANES) / LANES
    c, s = np.cos(phi), np.sin(phi)
    inner = np.block([[c, -s], [s, c]])
    twist = 2.0 * np.pi * k1[:, None] * q[None, :] / length
    twiddle = np.stack([np.cos(twist), -np.sin(twist)]).astype(np.float32)
    scale = 2.0 / length
    return (
        np.concatenate(halves(outer), axis=0),
        np.concatenate(halves(inner) + halves(inner.T), axis=0),
        np.concatenate(halves(outer.T * scale), axis=0),
        twiddle,
    )


def exchange_table(rows):
    table = np.zeros((GROUP, rows, rows, GROUP), np.float32)
    for e in range(GROUP):
        for r in range(rows):
            table[e, r, r, e] = 1.0
    return table.reshape(GROUP * rows, rows * GROUP).astype(ml_dtypes.bfloat16)


def dot(left, right, dims=((1,), (0,))):
    return lax.dot_general(left, right, (dims, ((), ())), preferred_element_type=F32)


def split_up(value):
    high = value.astype(BF16)
    return high, (value - high.astype(F32)).astype(BF16)


def dot3_left(table_high, table_low, value):
    high, low = split_up(value)
    return dot(table_high, high) + (dot(table_high, low) + dot(table_low, high))


def dot3_right(value, table_high, table_low):
    high, low = split_up(value)
    return dot(high, table_high) + (dot(low, table_high) + dot(high, table_low))


def write_messages(out_ref, swap, blocks):
    size = swap.shape[0]
    for g, block in enumerate(blocks):
        rows = jnp.concatenate(block, axis=0)
        out_ref[g * size : (g + 1) * size, :] = dot(swap, rows).astype(BF16)


def read_messages(in_ref, swap):
    size = swap.shape[0]
    return [
        dot(swap, in_ref[g * size : (g + 1) * size, :], ((0,), (0,))).astype(BF16)
        for g in range(64 // GROUP)
    ]


def lane_blocks(value):
    return [value[:, u * LANES : (u + 1) * LANES] for u in range(value.shape[1] // LANES)]


def by_run(values):
    parts = [x for value in values for x in lane_blocks(value)]
    return [[x[g * GROUP : (g + 1) * GROUP] for x in parts] for g in range(64 // GROUP)]


def whole_signal(groups, k):
    return jnp.concatenate([x[k * 64 : (k + 1) * 64] for x in groups], axis=0)


def pack_kernel(in_ref, grad_ref, *refs):
    *sources, own_ref, first, second, third, fourth, fifth, sem = refs
    pairs = [(in_ref, own_ref.at[pl.ds(0, 64), :]), (grad_ref, own_ref.at[pl.ds(64, 64), :])]
    pairs += zip(sources, (first, second, third, fourth, fifth))
    copies = [pltpu.make_async_copy(a, b, sem) for a, b in pairs]
    for copy in copies:
        copy.start()
    for copy in copies:
        copy.wait()


def project_kernel(
    ch_ref, own_ref, got1_ref, got3_ref, got2_ref, wv_ref, wg_ref, wo_ref, taps_ref, swap_ref,
    msg_ref, gate_ref, dgated_ref, in_ref, grad_ref,
):
    ch = ch_ref[0]
    for shift, ref in ((0, own_ref), (1, got1_ref), (3, got3_ref), (2, got2_ref)):
        at = pl.multiple_of(lax.rem(ch + (4 - shift), 4) * 64, 64)
        in_ref[pl.ds(at, 64), :] = ref[:64, :]
        grad_ref[pl.ds(at, 64), :] = ref[64:, :]
    full_in = in_ref[...]
    value = dot(wv_ref[...], full_in).astype(BF16)
    gate = dot(wg_ref[...], full_in)
    d_gated = dot(wo_ref[...], grad_ref[...])
    gate_ref[...] = gate
    dgated_ref[...] = d_gated
    d_mixed = (d_gated * gate).astype(BF16)
    signals = (value, d_mixed, *split_up(taps_ref[...]))
    write_messages(msg_ref, swap_ref[...], by_run(signals))


def spectrum(first, tw_re, tw_im, table_high, table_low):
    half = first.shape[0] // 2
    re, im = first[:half], first[half:]
    z = jnp.concatenate([re * tw_re - im * tw_im, re * tw_im + im * tw_re], axis=1)
    return dot3_right(z, table_high, table_low)


def convolve_kernel(got_ref, swap_ref, outer_ref, inner_ref, last_ref, tw_ref, out_ref):
    rows = outer_ref.shape[0] // 2
    size = 2 * LANES
    ih, il, jh, jl = (inner_ref[k * size : (k + 1) * size, :] for k in range(4))
    groups = read_messages(got_ref, swap_ref[...])
    v, d, high, low = (whole_signal(groups, k) for k in range(4))
    first = dot(outer_ref[:rows, :], jnp.concatenate([v, d, high, low], axis=1))
    more = dot(outer_ref[rows:, :], jnp.concatenate([v, d, high], axis=1))
    tw_re, tw_im = tw_ref[0], tw_ref[1]
    firsts, mores = lane_blocks(first), lane_blocks(more)
    firsts = [firsts[0] + mores[0], firsts[1] + mores[1], firsts[2] + firsts[3] + mores[2]]
    v, d, h = (lane_blocks(spectrum(x, tw_re, tw_im, ih, il)) for x in firsts)
    (v_re, v_im), (d_re, d_im), (h_re, h_im) = v, d, h
    products = (
        (h_re * v_re - h_im * v_im, h_re * v_im + h_im * v_re),
        (h_re * d_re + h_im * d_im, h_re * d_im - h_im * d_re),
        (v_re * d_re + v_im * d_im, v_re * d_im - v_im * d_re),
    )
    back = []
    for re, im in products:
        y = dot3_right(jnp.concatenate([re, im], axis=1), jh, jl)
        re, im = lane_blocks(y)
        b = jnp.concatenate([re * tw_re + im * tw_im, im * tw_re - re * tw_im], axis=0)
        back.append(dot3_left(last_ref[: rows // 2, :], last_ref[rows // 2 :, :], b))
    mixed, d_value, d_filter = back
    signals = (mixed.astype(BF16), d_value.astype(BF16), *split_up(d_filter))
    blocks = [[x[g * 64 : (g + 1) * 64] for x in signals] for g in range(64 // GROUP)]
    write_messages(out_ref, swap_ref[...], blocks)


def gradient_kernel(
    ch_ref, got_ref, swap_ref, gate_ref, dgated_ref, in_ref, grad_ref, wv_ref, wg_ref,
    sums_ref, own_ref, send1_ref, send3_ref, send2_ref, filt_ref, part_ref, *, scale
):
    groups = read_messages(got_ref, swap_ref[...])

    def signal(k):
        cols = []
        for u in range(4):
            at = (k * 4 + u) * GROUP
            cols.append(jnp.concatenate([x[at : at + GROUP] for x in groups], axis=0))
        return jnp.concatenate(cols, axis=1)

    mixed = signal(0).astype(F32)
    d_value = signal(1)
    filt_ref[...] = (signal(2).astype(F32) + signal(3).astype(F32)) * scale
    gated_out = (gate_ref[...] * mixed).astype(BF16)
    d_gate = (dgated_ref[...] * mixed).astype(BF16)
    both = jnp.concatenate([d_value, d_gate], axis=0)
    weights = jnp.concatenate([wv_ref[...], wg_ref[...]], axis=0)
    part_ref[...] = dot(weights, both, ((0,), (0,)))
    ch = ch_ref[0]

    def block(shift):
        at = pl.multiple_of(lax.rem(ch + shift, 4) * 64, 64)
        return part_ref[pl.ds(at, 64), :]

    own_ref[...] = block(0)
    send1_ref[...] = block(1).astype(BF16)
    send3_ref[...] = block(3).astype(BF16)
    send2_ref[...] = block(2).astype(BF16)
    term = dot(both, in_ref[...], ((1,), (1,)))
    out_term = dot(gated_out, grad_ref[...], ((1,), (1,)))
    tiles = []
    for value in (term, out_term):
        for a in range(value.shape[0] // 8):
            tiles += lane_blocks(value[8 * a : 8 * a + 8])
    tiles += [jnp.zeros_like(tiles[0])] * (64 - len(tiles))
    sums_ref[...] = jnp.concatenate(tiles, axis=0).astype(BF16)


def total_kernel(got_ref, out_ref, *, scale):
    total = got_ref[...].astype(F32).reshape(64, 8, LANES).sum(axis=0) * scale
    whole = jnp.broadcast_to(total[None], (64, 8, LANES)).reshape(512, LANES)
    out_ref[...] = whole.astype(BF16)


def settle_kernel(
    got_ref, own_ref, came1_ref, came3_ref, came2_ref, din_ref, dwv_ref, dwg_ref, dwo_ref
):
    d_inputs = own_ref[...]
    for ref in (came1_ref, came3_ref, came2_ref):
        d_inputs = d_inputs + ref[...].astype(F32)
    din_ref[...] = d_inputs.astype(BF16)
    for k, ref in enumerate((dwv_ref, dwg_ref, dwo_ref)):
        for a in range(8):
            at = 16 * (8 * k + a)
            pair = got_ref[at : at + 16, :].astype(F32)
            ref[8 * a : 8 * a + 8, :] = jnp.concatenate([pair[:8], pair[8:]], axis=1)


ANY = pl.BlockSpec(memory_space=pl.ANY)
VMEM = pl.BlockSpec(memory_space=pltpu.VMEM)
SMEM = pl.BlockSpec(memory_space=pltpu.SMEM)


def near(value):
    return pltpu.with_memory_space_constraint(value, pltpu.VMEM)


def far(value):
    return pltpu.with_memory_space_constraint(value, pltpu.HBM)


def call(kernel, outs, *args, scalar=None, scratch=()):
    many = isinstance(outs, list)
    specs = [VMEM] * len(args)
    args = [near(x) for x in args]
    if scalar is not None:
        specs, args = ([SMEM] + specs, [scalar] + args)
    return pl.pallas_call(
        kernel,
        out_shape=tuple(outs) if many else outs,
        in_specs=specs,
        out_specs=(VMEM,) * len(outs) if many else VMEM,
        scratch_shapes=scratch,
        compiler_params=pltpu.CompilerParams(vmem_limit_bytes=16 << 20),
    )(*args)


def packed(inputs, grad_out, *rest):
    outs = [pltpu.VMEM((2 * inputs.shape[0], inputs.shape[1]), inputs.dtype)]
    outs += [pltpu.VMEM(x.shape, x.dtype) for x in rest]
    return pl.pallas_call(
        pack_kernel,
        out_shape=tuple(outs),
        in_specs=[ANY] * (2 + len(rest)),
        out_specs=(VMEM,) * len(outs),
        scratch_shapes=[pltpu.SemaphoreType.DMA(())],
        compiler_params=pltpu.CompilerParams(vmem_limit_bytes=16 << 20),
        name="pack",
    )(*[far(x) for x in (inputs, grad_out, *rest)])


def exchanged(rows, axis):
    count = lax.axis_size(axis)
    parts = rows.reshape(count, rows.shape[0] // count, rows.shape[1])
    return lax.all_to_all(parts, axis, 0, 0, tiled=True).reshape(rows.shape)


def shifted(value, shift):
    return lax.ppermute(value, "ch", [(i, (i + shift) % 4) for i in range(4)])


def on_device(inputs, w_value, w_gate, w_out, filter_taps, grad_out):
    tokens = filter_taps.shape[1] * lax.axis_size("seq")
    scale = 1.0 / math.sqrt(tokens)
    outer, inner, last, twiddle = [jnp.asarray(t) for t in transform_tables(tokens)]
    swap = jnp.asarray(exchange_table(16))
    ch = lax.axis_index("ch").astype(jnp.int32).reshape(1)
    inside = pltpu.VMEM
    outside = jax.ShapeDtypeStruct

    own, wv, wg, wo, taps, tw = packed(
        inputs, grad_out, w_value.T, w_gate.T, w_out, filter_taps, twiddle
    )
    got = [shifted(own, s) for s in (1, 3, 2)]
    msg, gate, d_gated, full_in, full_grad = call(
        project_kernel,
        [
            inside((1024, LANES), BF16),
            inside((64, 512), F32),
            inside((64, 512), F32),
            inside((256, 512), BF16),
            inside((256, 512), BF16),
        ],
        own, *got, wv, wg, wo, taps, swap, scalar=ch,
    )
    back = call(
        convolve_kernel, inside((1024, LANES), BF16),
        exchanged(msg, "seq"), swap, outer, inner, last, tw,
    )
    sums, mine, send1, send3, send2, d_filter = call(
        lambda *refs: gradient_kernel(*refs, scale=scale),
        [
            inside((512, LANES), BF16),
            inside((64, 512), F32),
            inside((64, 512), BF16),
            inside((64, 512), BF16),
            inside((64, 512), BF16),
            outside((64, 512), F32),
        ],
        exchanged(back, "seq"), swap, gate, d_gated, full_in, full_grad, wv, wg,
        scalar=ch, scratch=[pltpu.VMEM((256, 512), F32)],
    )
    arrived = exchanged(sums, "seq")
    came = [shifted(x, s) for x, s in ((send2, 2), (send3, 3), (send1, 1))]
    total = call(
        lambda *refs: total_kernel(*refs, scale=scale),
        inside((512, LANES), BF16), arrived,
    )
    d_inputs, dwv, dwg, dwo = call(
        settle_kernel,
        [outside((64, 512), BF16)] + [outside((64, 256), F32)] * 3,
        exchanged(total, "seq"), mine, *came,
    )
    return d_inputs, dwv.T, dwg.T, dwo, d_filter


def solution(mesh):
    placed = (
        P("ch", "seq"),
        P(None, "ch"),
        P(None, "ch"),
        P("ch", None),
        P("ch", "seq"),
        P("ch", "seq"),
    )
    return jax.shard_map(
        on_device,
        mesh=mesh,
        in_specs=placed,
        out_specs=(P("ch", "seq"), P(None, "ch"), P(None, "ch"), P("ch", None), P("ch", "seq")),
        check_vma=False,
    )
```

```python
import math

import jax
import jax.numpy as jnp
import ml_dtypes
import numpy as np
from jax import lax
from jax.experimental import pallas as pl
from jax.experimental.pallas import tpu as pltpu
from jax.sharding import PartitionSpec as P


F32 = jnp.float32
BF16 = jnp.bfloat16
LANES = 128
GROUP = 16


def halves(table):
    high = table.astype(ml_dtypes.bfloat16)
    low = (table - high.astype(np.float64)).astype(ml_dtypes.bfloat16)
    return high, low


def transform_tables(tokens):
    rows = tokens // LANES
    length = 2 * tokens
    per_sender = rows // 64
    order = np.arange(rows).reshape(64 // GROUP, GROUP, per_sender)
    order = order.transpose(0, 2, 1).reshape(-1)
    k1 = np.arange(rows) + 0.5
    theta = 2.0 * np.pi * ((k1[:, None] * order[None, :]) % (2 * rows)) / (2 * rows)
    outer = np.concatenate([np.cos(theta), -np.sin(theta)], axis=0)
    q = np.arange(LANES)
    phi = 2.0 * np.pi * ((q[:, None] * q[None, :]) % LANES) / LANES
    c, s = np.cos(phi), np.sin(phi)
    inner = np.block([[c, -s], [s, c]])
    twist = 2.0 * np.pi * k1[:, None] * q[None, :] / length
    twiddle = np.stack([np.cos(twist), -np.sin(twist)]).astype(np.float32)
    scale = 2.0 / length
    return (
        np.concatenate(halves(outer), axis=0),
        np.concatenate(halves(inner) + halves(inner.T), axis=0),
        np.concatenate(halves(outer.T * scale), axis=0),
        twiddle,
    )


def exchange_table(rows):
    table = np.zeros((GROUP, rows, rows, GROUP), np.float32)
    for e in range(GROUP):
        for r in range(rows):
            table[e, r, r, e] = 1.0
    return table.reshape(GROUP * rows, rows * GROUP).astype(ml_dtypes.bfloat16)


def dot(left, right, dims=((1,), (0,))):
    return lax.dot_general(left, right, (dims, ((), ())), preferred_element_type=F32)


def split_up(value):
    high = value.astype(BF16)
    return high, (value - high.astype(F32)).astype(BF16)


def dot_left(table_high, table_low, value):
    value = value.astype(BF16)
    return dot(table_high, value) + dot(table_low, value)


def dot_right(value, table_high, table_low):
    value = value.astype(BF16)
    return dot(value, table_high) + dot(value, table_low)


def write_messages(out_ref, swap, blocks):
    size = swap.shape[0]
    for g, block in enumerate(blocks):
        rows = jnp.concatenate(block, axis=0)
        out_ref[g * size : (g + 1) * size, :] = dot(swap, rows).astype(BF16)


def read_messages(in_ref, swap):
    size = swap.shape[0]
    return [
        dot(swap, in_ref[g * size : (g + 1) * size, :], ((0,), (0,))).astype(BF16)
        for g in range(64 // GROUP)
    ]


def lane_blocks(value):
    return [value[:, u * LANES : (u + 1) * LANES] for u in range(value.shape[1] // LANES)]


def by_run(values):
    parts = [x for value in values for x in lane_blocks(value)]
    return [[x[g * GROUP : (g + 1) * GROUP] for x in parts] for g in range(64 // GROUP)]


def whole_signal(groups, k):
    return jnp.concatenate([x[k * 64 : (k + 1) * 64] for x in groups], axis=0)


def pack_kernel(in_ref, grad_ref, own_ref, sem):
    half = own_ref.shape[0] // 2
    copies = [
        pltpu.make_async_copy(in_ref, own_ref.at[pl.ds(0, half), :], sem),
        pltpu.make_async_copy(grad_ref, own_ref.at[pl.ds(half, half), :], sem),
    ]
    for copy in copies:
        copy.start()
    for copy in copies:
        copy.wait()


def fetch_kernel(*refs):
    *refs, sem = refs
    count = len(refs) // 2
    copies = [pltpu.make_async_copy(a, b, sem) for a, b in zip(refs[:count], refs[count:])]
    for copy in copies:
        copy.start()
    for copy in copies:
        copy.wait()


def project_kernel(
    ch_ref, own_ref, got1_ref, got3_ref, got2_ref, wv_ref, wg_ref, wo_ref, taps_ref, swap_ref,
    msg_ref, gate_ref, dgated_ref, in_ref, grad_ref,
):
    ch = ch_ref[0]
    for shift, ref in ((0, own_ref), (1, got1_ref), (3, got3_ref), (2, got2_ref)):
        at = pl.multiple_of(lax.rem(ch + (4 - shift), 4) * 64, 64)
        in_ref[pl.ds(at, 64), :] = ref[:64, :]
        grad_ref[pl.ds(at, 64), :] = ref[64:, :]
    full_in = in_ref[...]
    value = dot(wv_ref[...], full_in).astype(BF16)
    gate = dot(wg_ref[...], full_in)
    d_gated = dot(wo_ref[...], grad_ref[...])
    gate_ref[...] = gate
    dgated_ref[...] = d_gated
    d_mixed = (d_gated * gate).astype(BF16)
    signals = (value, d_mixed, *split_up(taps_ref[...]))
    write_messages(msg_ref, swap_ref[...], by_run(signals))


def spectrum(first, tw_re, tw_im, table_high, table_low):
    half = first.shape[0] // 2
    re, im = first[:half], first[half:]
    z = jnp.concatenate([re * tw_re - im * tw_im, re * tw_im + im * tw_re], axis=1)
    return dot_right(z, table_high, table_low)


def convolve_kernel(got_ref, swap_ref, outer_ref, inner_ref, last_ref, tw_ref, out_ref):
    rows = outer_ref.shape[0] // 2
    size = 2 * LANES
    ih, il, jh, jl = (inner_ref[k * size : (k + 1) * size, :] for k in range(4))
    groups = read_messages(got_ref, swap_ref[...])
    v, d, high, low = (whole_signal(groups, k) for k in range(4))
    first = dot(outer_ref[:rows, :], jnp.concatenate([v, d, high, low], axis=1))
    more = dot(outer_ref[rows:, :], jnp.concatenate([v, d, high], axis=1))
    tw_re, tw_im = tw_ref[0], tw_ref[1]
    firsts, mores = lane_blocks(first), lane_blocks(more)
    firsts = [firsts[0] + mores[0], firsts[1] + mores[1], firsts[2] + firsts[3] + mores[2]]
    v, d, h = (lane_blocks(spectrum(x, tw_re, tw_im, ih, il)) for x in firsts)
    (v_re, v_im), (d_re, d_im), (h_re, h_im) = v, d, h
    products = (
        (h_re * v_re - h_im * v_im, h_re * v_im + h_im * v_re),
        (h_re * d_re + h_im * d_im, h_re * d_im - h_im * d_re),
        (v_re * d_re + v_im * d_im, v_re * d_im - v_im * d_re),
    )
    back = []
    for re, im in products:
        y = dot_right(jnp.concatenate([re, im], axis=1), jh, jl)
        re, im = lane_blocks(y)
        b = jnp.concatenate([re * tw_re + im * tw_im, im * tw_re - re * tw_im], axis=0)
        back.append(dot_left(last_ref[: rows // 2, :], last_ref[rows // 2 :, :], b))
    mixed, d_value, d_filter = back
    signals = (mixed.astype(BF16), d_value.astype(BF16), *split_up(d_filter))
    blocks = [[x[g * 64 : (g + 1) * 64] for x in signals] for g in range(64 // GROUP)]
    write_messages(out_ref, swap_ref[...], blocks)


def gradient_kernel(
    ch_ref, got_ref, swap_ref, gate_ref, dgated_ref, in_ref, grad_ref, wv_ref, wg_ref,
    sums_ref, own_ref, send1_ref, send3_ref, send2_ref, filt_ref, part_ref, *, scale
):
    groups = read_messages(got_ref, swap_ref[...])

    def signal(k):
        cols = []
        for u in range(4):
            at = (k * 4 + u) * GROUP
            cols.append(jnp.concatenate([x[at : at + GROUP] for x in groups], axis=0))
        return jnp.concatenate(cols, axis=1)

    mixed = signal(0).astype(F32)
    d_value = signal(1)
    filt_ref[...] = (signal(2).astype(F32) + signal(3).astype(F32)) * scale
    gated_out = (gate_ref[...] * mixed).astype(BF16)
    d_gate = (dgated_ref[...] * mixed).astype(BF16)
    both = jnp.concatenate([d_value, d_gate], axis=0)
    weights = jnp.concatenate([wv_ref[...], wg_ref[...]], axis=0)
    part_ref[...] = dot(weights, both, ((0,), (0,)))
    ch = ch_ref[0]

    def block(shift):
        at = pl.multiple_of(lax.rem(ch + shift, 4) * 64, 64)
        return part_ref[pl.ds(at, 64), :]

    own_ref[...] = block(0)
    send1_ref[...] = block(1).astype(BF16)
    send3_ref[...] = block(3).astype(BF16)
    send2_ref[...] = block(2).astype(BF16)
    term = dot(both, in_ref[...], ((1,), (1,)))
    out_term = dot(gated_out, grad_ref[...], ((1,), (1,)))
    tiles = []
    for value in (term, out_term):
        for a in range(value.shape[0] // 8):
            tiles += lane_blocks(value[8 * a : 8 * a + 8])
    tiles += [jnp.zeros_like(tiles[0])] * (64 - len(tiles))
    sums_ref[...] = jnp.concatenate(tiles, axis=0).astype(BF16)


def total_kernel(got_ref, out_ref, *, scale):
    total = got_ref[...].astype(F32).reshape(64, 8, LANES).sum(axis=0) * scale
    whole = jnp.broadcast_to(total[None], (64, 8, LANES)).reshape(512, LANES)
    out_ref[...] = whole.astype(BF16)


def settle_kernel(
    got_ref, own_ref, came1_ref, came3_ref, came2_ref, din_ref, dwv_ref, dwg_ref, dwo_ref
):
    d_inputs = own_ref[...]
    for ref in (came1_ref, came3_ref, came2_ref):
        d_inputs = d_inputs + ref[...].astype(F32)
    din_ref[...] = d_inputs.astype(BF16)
    for k, ref in enumerate((dwv_ref, dwg_ref, dwo_ref)):
        for a in range(8):
            at = 16 * (8 * k + a)
            pair = got_ref[at : at + 16, :].astype(F32)
            ref[8 * a : 8 * a + 8, :] = jnp.concatenate([pair[:8], pair[8:]], axis=1)


ANY = pl.BlockSpec(memory_space=pl.ANY)
VMEM = pl.BlockSpec(memory_space=pltpu.VMEM)
SMEM = pl.BlockSpec(memory_space=pltpu.SMEM)


def near(value):
    return pltpu.with_memory_space_constraint(value, pltpu.VMEM)


def far(value):
    return pltpu.with_memory_space_constraint(value, pltpu.HBM)


def call(kernel, outs, *args, scalar=None, scratch=()):
    many = isinstance(outs, list)
    specs = [VMEM] * len(args)
    args = [near(x) for x in args]
    if scalar is not None:
        specs, args = ([SMEM] + specs, [scalar] + args)
    return pl.pallas_call(
        kernel,
        out_shape=tuple(outs) if many else outs,
        in_specs=specs,
        out_specs=(VMEM,) * len(outs) if many else VMEM,
        scratch_shapes=scratch,
        compiler_params=pltpu.CompilerParams(vmem_limit_bytes=16 << 20),
    )(*args)


def copied(kernel, outs, *args):
    return pl.pallas_call(
        kernel,
        out_shape=tuple(outs),
        in_specs=[ANY] * len(args),
        out_specs=(VMEM,) * len(outs),
        scratch_shapes=[pltpu.SemaphoreType.DMA(())],
        compiler_params=pltpu.CompilerParams(vmem_limit_bytes=16 << 20),
    )(*[far(x) for x in args])


def exchanged(rows, axis):
    count = lax.axis_size(axis)
    parts = rows.reshape(count, rows.shape[0] // count, rows.shape[1])
    return lax.all_to_all(parts, axis, 0, 0, tiled=True).reshape(rows.shape)


def shifted(value, shift):
    return lax.ppermute(value, "ch", [(i, (i + shift) % 4) for i in range(4)])


def on_device(inputs, w_value, w_gate, w_out, filter_taps, grad_out):
    tokens = filter_taps.shape[1] * lax.axis_size("seq")
    scale = 1.0 / math.sqrt(tokens)
    outer, inner, last, twiddle = [jnp.asarray(t) for t in transform_tables(tokens)]
    swap = jnp.asarray(exchange_table(16))
    ch = lax.axis_index("ch").astype(jnp.int32).reshape(1)
    inside = pltpu.VMEM
    outside = jax.ShapeDtypeStruct

    rows, length = inputs.shape
    (own,) = copied(pack_kernel, [inside((2 * rows, length), inputs.dtype)], inputs, grad_out)
    later = (w_value.T, w_gate.T, w_out, filter_taps, twiddle)
    got = [shifted(own, s) for s in (1, 3, 2)]
    wv, wg, wo, taps, tw = copied(fetch_kernel, [inside(x.shape, x.dtype) for x in later], *later)
    msg, gate, d_gated, full_in, full_grad = call(
        project_kernel,
        [
            inside((1024, LANES), BF16),
            inside((64, 512), F32),
            inside((64, 512), F32),
            inside((256, 512), BF16),
            inside((256, 512), BF16),
        ],
        own, *got, wv, wg, wo, taps, swap, scalar=ch,
    )
    back = call(
        convolve_kernel, inside((1024, LANES), BF16),
        exchanged(msg, "seq"), swap, outer, inner, last, tw,
    )
    sums, mine, send1, send3, send2, d_filter = call(
        lambda *refs: gradient_kernel(*refs, scale=scale),
        [
            inside((512, LANES), BF16),
            inside((64, 512), F32),
            inside((64, 512), BF16),
            inside((64, 512), BF16),
            inside((64, 512), BF16),
            outside((64, 512), F32),
        ],
        exchanged(back, "seq"), swap, gate, d_gated, full_in, full_grad, wv, wg,
        scalar=ch, scratch=[pltpu.VMEM((256, 512), F32)],
    )
    arrived = exchanged(sums, "seq")
    came2, came1 = shifted(send2, 2), shifted(send1, 1)
    total = call(
        lambda *refs: total_kernel(*refs, scale=scale),
        inside((512, LANES), BF16), arrived,
    )
    spread = exchanged(total, "seq")
    came3 = shifted(send3, 3)
    d_inputs, dwv, dwg, dwo = call(
        settle_kernel,
        [outside((64, 512), BF16)] + [outside((64, 256), F32)] * 3,
        spread, mine, came1, came3, came2,
    )
    return d_inputs, dwv.T, dwg.T, dwo, d_filter


def solution(mesh):
    placed = (
        P("ch", "seq"),
        P(None, "ch"),
        P(None, "ch"),
        P("ch", None),
        P("ch", "seq"),
        P("ch", "seq"),
    )
    return jax.shard_map(
        on_device,
        mesh=mesh,
        in_specs=placed,
        out_specs=(P("ch", "seq"), P(None, "ch"), P(None, "ch"), P("ch", None), P("ch", "seq")),
        check_vma=False,
    )
```

```python
import math

import jax
import jax.numpy as jnp
import ml_dtypes
import numpy as np
from jax import lax
from jax.experimental import pallas as pl
from jax.experimental.pallas import tpu as pltpu
from jax.sharding import PartitionSpec as P


F32 = jnp.float32
BF16 = jnp.bfloat16
LANES = 128
GROUP = 16


def halves(table):
    high = table.astype(ml_dtypes.bfloat16)
    low = (table - high.astype(np.float64)).astype(ml_dtypes.bfloat16)
    return high, low


def transform_tables(tokens):
    rows = tokens // LANES
    length = 2 * tokens
    per_sender = rows // 64
    order = np.arange(rows).reshape(64 // GROUP, GROUP, per_sender)
    order = order.transpose(0, 2, 1).reshape(-1)
    k1 = np.arange(rows) + 0.5
    theta = 2.0 * np.pi * ((k1[:, None] * order[None, :]) % (2 * rows)) / (2 * rows)
    outer = np.concatenate([np.cos(theta), -np.sin(theta)], axis=0)
    q = np.arange(LANES)
    phi = 2.0 * np.pi * ((q[:, None] * q[None, :]) % LANES) / LANES
    c, s = np.cos(phi), np.sin(phi)
    inner = np.block([[c, -s], [s, c]])
    twist = 2.0 * np.pi * k1[:, None] * q[None, :] / length
    twiddle = np.stack([np.cos(twist), -np.sin(twist)]).astype(np.float32)
    scale = 2.0 / length
    return (
        np.concatenate(halves(outer), axis=0),
        np.concatenate(halves(inner) + halves(inner.T), axis=0),
        np.concatenate(halves(outer.T * scale), axis=0),
        twiddle,
    )


def exchange_table(rows):
    table = np.zeros((GROUP, rows, rows, GROUP), np.float32)
    for e in range(GROUP):
        for r in range(rows):
            table[e, r, r, e] = 1.0
    return table.reshape(GROUP * rows, rows * GROUP).astype(ml_dtypes.bfloat16)


def dot(left, right, dims=((1,), (0,))):
    return lax.dot_general(left, right, (dims, ((), ())), preferred_element_type=F32)


def split_up(value):
    high = value.astype(BF16)
    return high, (value - high.astype(F32)).astype(BF16)


def dot_left(table_high, table_low, value):
    value = value.astype(BF16)
    return dot(table_high, value) + dot(table_low, value)


def dot_right(value, table_high, table_low):
    value = value.astype(BF16)
    return dot(value, table_high) + dot(value, table_low)


def write_messages(out_ref, swap, blocks):
    size = swap.shape[0]
    for g, block in enumerate(blocks):
        rows = jnp.concatenate(block, axis=0)
        out_ref[g * size : (g + 1) * size, :] = dot(swap, rows).astype(BF16)


def read_messages(in_ref, swap):
    size = swap.shape[0]
    return [
        dot(swap, in_ref[g * size : (g + 1) * size, :], ((0,), (0,))).astype(BF16)
        for g in range(64 // GROUP)
    ]


def lane_blocks(value):
    return [value[:, u * LANES : (u + 1) * LANES] for u in range(value.shape[1] // LANES)]


def by_run(values):
    parts = [x for value in values for x in lane_blocks(value)]
    return [[x[g * GROUP : (g + 1) * GROUP] for x in parts] for g in range(64 // GROUP)]


def whole_signal(groups, k):
    return jnp.concatenate([x[k * 64 : (k + 1) * 64] for x in groups], axis=0)


def pack_kernel(in_ref, grad_ref, own_ref, sem):
    half = own_ref.shape[0] // 2
    copies = [
        pltpu.make_async_copy(in_ref, own_ref.at[pl.ds(0, half), :], sem),
        pltpu.make_async_copy(grad_ref, own_ref.at[pl.ds(half, half), :], sem),
    ]
    for copy in copies:
        copy.start()
    for copy in copies:
        copy.wait()


def fetch_kernel(*refs):
    *refs, sem = refs
    count = len(refs) // 2
    copies = [pltpu.make_async_copy(a, b, sem) for a, b in zip(refs[:count], refs[count:])]
    for copy in copies:
        copy.start()
    for copy in copies:
        copy.wait()


def project_kernel(
    ch_ref, own_ref, got1_ref, got3_ref, got2_ref, wv_ref, wg_ref, wo_ref, taps_ref, swap_ref,
    msg_ref, gate_ref, dgated_ref, in_ref, grad_ref,
):
    ch = ch_ref[0]
    for shift, ref in ((0, own_ref), (1, got1_ref), (3, got3_ref), (2, got2_ref)):
        at = pl.multiple_of((ch ^ shift) * 64, 64)
        in_ref[pl.ds(at, 64), :] = ref[:64, :]
        grad_ref[pl.ds(at, 64), :] = ref[64:, :]
    full_in = in_ref[...]
    value = dot(wv_ref[...], full_in).astype(BF16)
    gate = dot(wg_ref[...], full_in)
    d_gated = dot(wo_ref[...], grad_ref[...])
    gate_ref[...] = gate
    dgated_ref[...] = d_gated
    d_mixed = (d_gated * gate).astype(BF16)
    signals = (value, d_mixed, *split_up(taps_ref[...]))
    write_messages(msg_ref, swap_ref[...], by_run(signals))


def spectrum(first, tw_re, tw_im, table_high, table_low):
    half = first.shape[0] // 2
    re, im = first[:half], first[half:]
    z = jnp.concatenate([re * tw_re - im * tw_im, re * tw_im + im * tw_re], axis=1)
    return dot_right(z, table_high, table_low)


def convolve_kernel(got_ref, swap_ref, outer_ref, inner_ref, last_ref, tw_ref, out_ref):
    rows = outer_ref.shape[0] // 2
    size = 2 * LANES
    ih, il, jh, jl = (inner_ref[k * size : (k + 1) * size, :] for k in range(4))
    groups = read_messages(got_ref, swap_ref[...])
    v, d, high, low = (whole_signal(groups, k) for k in range(4))
    first = dot(outer_ref[:rows, :], jnp.concatenate([v, d, high, low], axis=1))
    more = dot(outer_ref[rows:, :], jnp.concatenate([v, d, high], axis=1))
    tw_re, tw_im = tw_ref[0], tw_ref[1]
    firsts, mores = lane_blocks(first), lane_blocks(more)
    firsts = [firsts[0] + mores[0], firsts[1] + mores[1], firsts[2] + firsts[3] + mores[2]]
    v, d, h = (lane_blocks(spectrum(x, tw_re, tw_im, ih, il)) for x in firsts)
    (v_re, v_im), (d_re, d_im), (h_re, h_im) = v, d, h
    products = (
        (h_re * v_re - h_im * v_im, h_re * v_im + h_im * v_re),
        (h_re * d_re + h_im * d_im, h_re * d_im - h_im * d_re),
        (v_re * d_re + v_im * d_im, v_re * d_im - v_im * d_re),
    )
    back = []
    for re, im in products:
        y = dot_right(jnp.concatenate([re, im], axis=1), jh, jl)
        re, im = lane_blocks(y)
        b = jnp.concatenate([re * tw_re + im * tw_im, im * tw_re - re * tw_im], axis=0)
        back.append(dot_left(last_ref[: rows // 2, :], last_ref[rows // 2 :, :], b))
    mixed, d_value, d_filter = back
    signals = (mixed.astype(BF16), d_value.astype(BF16), *split_up(d_filter))
    blocks = [[x[g * 64 : (g + 1) * 64] for x in signals] for g in range(64 // GROUP)]
    write_messages(out_ref, swap_ref[...], blocks)


def gradient_kernel(
    ch_ref, got_ref, swap_ref, gate_ref, dgated_ref, in_ref, grad_ref, wv_ref, wg_ref,
    sums_ref, own_ref, send1_ref, send3_ref, send2_ref, filt_ref, part_ref, *, scale
):
    groups = read_messages(got_ref, swap_ref[...])

    def signal(k):
        cols = []
        for u in range(4):
            at = (k * 4 + u) * GROUP
            cols.append(jnp.concatenate([x[at : at + GROUP] for x in groups], axis=0))
        return jnp.concatenate(cols, axis=1)

    mixed = signal(0).astype(F32)
    d_value = signal(1)
    filt_ref[...] = (signal(2).astype(F32) + signal(3).astype(F32)) * scale
    gated_out = (gate_ref[...] * mixed).astype(BF16)
    d_gate = (dgated_ref[...] * mixed).astype(BF16)
    both = jnp.concatenate([d_value, d_gate], axis=0)
    weights = jnp.concatenate([wv_ref[...], wg_ref[...]], axis=0)
    part_ref[...] = dot(weights, both, ((0,), (0,)))
    ch = ch_ref[0]

    def block(shift):
        at = pl.multiple_of((ch ^ shift) * 64, 64)
        return part_ref[pl.ds(at, 64), :]

    own_ref[...] = block(0)
    send1_ref[...] = block(1).astype(BF16)
    send3_ref[...] = block(3).astype(BF16)
    send2_ref[...] = block(2).astype(BF16)
    term = dot(both, in_ref[...], ((1,), (1,)))
    out_term = dot(gated_out, grad_ref[...], ((1,), (1,)))
    tiles = []
    for value in (term, out_term):
        for a in range(value.shape[0] // 8):
            tiles += lane_blocks(value[8 * a : 8 * a + 8])
    tiles += [jnp.zeros_like(tiles[0])] * (64 - len(tiles))
    sums_ref[...] = jnp.concatenate(tiles, axis=0).astype(BF16)


def total_kernel(got_ref, out_ref, *, scale):
    total = got_ref[...].astype(F32).reshape(64, 8, LANES).sum(axis=0) * scale
    whole = jnp.broadcast_to(total[None], (64, 8, LANES)).reshape(512, LANES)
    out_ref[...] = whole.astype(BF16)


def settle_kernel(
    got_ref, own_ref, came1_ref, came3_ref, came2_ref, din_ref, dwv_ref, dwg_ref, dwo_ref
):
    d_inputs = own_ref[...]
    for ref in (came1_ref, came3_ref, came2_ref):
        d_inputs = d_inputs + ref[...].astype(F32)
    din_ref[...] = d_inputs.astype(BF16)
    for k, ref in enumerate((dwv_ref, dwg_ref, dwo_ref)):
        for a in range(8):
            at = 16 * (8 * k + a)
            pair = got_ref[at : at + 16, :].astype(F32)
            ref[8 * a : 8 * a + 8, :] = jnp.concatenate([pair[:8], pair[8:]], axis=1)


ANY = pl.BlockSpec(memory_space=pl.ANY)
VMEM = pl.BlockSpec(memory_space=pltpu.VMEM)
SMEM = pl.BlockSpec(memory_space=pltpu.SMEM)


def near(value):
    return pltpu.with_memory_space_constraint(value, pltpu.VMEM)


def far(value):
    return pltpu.with_memory_space_constraint(value, pltpu.HBM)


def call(kernel, outs, *args, scalar=None, scratch=()):
    many = isinstance(outs, list)
    specs = [VMEM] * len(args)
    args = [near(x) for x in args]
    if scalar is not None:
        specs, args = ([SMEM] + specs, [scalar] + args)
    return pl.pallas_call(
        kernel,
        out_shape=tuple(outs) if many else outs,
        in_specs=specs,
        out_specs=(VMEM,) * len(outs) if many else VMEM,
        scratch_shapes=scratch,
        compiler_params=pltpu.CompilerParams(vmem_limit_bytes=16 << 20),
    )(*args)


def copied(kernel, outs, *args):
    return pl.pallas_call(
        kernel,
        out_shape=tuple(outs),
        in_specs=[ANY] * len(args),
        out_specs=(VMEM,) * len(outs),
        scratch_shapes=[pltpu.SemaphoreType.DMA(())],
        compiler_params=pltpu.CompilerParams(vmem_limit_bytes=16 << 20),
    )(*[far(x) for x in args])


def exchanged(rows, axis):
    count = lax.axis_size(axis)
    parts = rows.reshape(count, rows.shape[0] // count, rows.shape[1])
    return lax.all_to_all(parts, axis, 0, 0, tiled=True).reshape(rows.shape)


def shifted(value, shift):
    return lax.ppermute(value, "ch", [(i, i ^ shift) for i in range(4)])


def on_device(inputs, w_value, w_gate, w_out, filter_taps, grad_out):
    tokens = filter_taps.shape[1] * lax.axis_size("seq")
    scale = 1.0 / math.sqrt(tokens)
    outer, inner, last, twiddle = [jnp.asarray(t) for t in transform_tables(tokens)]
    swap = jnp.asarray(exchange_table(16))
    ch = lax.axis_index("ch").astype(jnp.int32).reshape(1)
    inside = pltpu.VMEM
    outside = jax.ShapeDtypeStruct

    rows, length = inputs.shape
    (own,) = copied(pack_kernel, [inside((2 * rows, length), inputs.dtype)], inputs, grad_out)
    later = (w_value.T, w_gate.T, w_out, filter_taps, twiddle)
    got = [shifted(own, s) for s in (1, 3)]
    got.append(shifted(own, 2))
    wv, wg, wo, taps, tw = copied(fetch_kernel, [inside(x.shape, x.dtype) for x in later], *later)
    msg, gate, d_gated, full_in, full_grad = call(
        project_kernel,
        [
            inside((1024, LANES), BF16),
            inside((64, 512), F32),
            inside((64, 512), F32),
            inside((256, 512), BF16),
            inside((256, 512), BF16),
        ],
        own, *got, wv, wg, wo, taps, swap, scalar=ch,
    )
    back = call(
        convolve_kernel, inside((1024, LANES), BF16),
        exchanged(msg, "seq"), swap, outer, inner, last, tw,
    )
    sums, mine, send1, send3, send2, d_filter = call(
        lambda *refs: gradient_kernel(*refs, scale=scale),
        [
            inside((512, LANES), BF16),
            inside((64, 512), F32),
            inside((64, 512), BF16),
            inside((64, 512), BF16),
            inside((64, 512), BF16),
            outside((64, 512), F32),
        ],
        exchanged(back, "seq"), swap, gate, d_gated, full_in, full_grad, wv, wg,
        scalar=ch, scratch=[pltpu.VMEM((256, 512), F32)],
    )
    arrived = exchanged(sums, "seq")
    came3, came1 = shifted(send3, 3), shifted(send1, 1)
    total = call(
        lambda *refs: total_kernel(*refs, scale=scale),
        inside((512, LANES), BF16), arrived,
    )
    spread = exchanged(total, "seq")
    came2 = shifted(send2, 2)
    d_inputs, dwv, dwg, dwo = call(
        settle_kernel,
        [outside((64, 512), BF16)] + [outside((64, 256), F32)] * 3,
        spread, mine, came1, came3, came2,
    )
    return d_inputs, dwv.T, dwg.T, dwo, d_filter


def solution(mesh):
    placed = (
        P("ch", "seq"),
        P(None, "ch"),
        P(None, "ch"),
        P("ch", None),
        P("ch", "seq"),
        P("ch", "seq"),
    )
    return jax.shard_map(
        on_device,
        mesh=mesh,
        in_specs=placed,
        out_specs=(P("ch", "seq"), P(None, "ch"), P(None, "ch"), P("ch", None), P("ch", "seq")),
        check_vma=False,
    )
```

```python
import math

import jax
import jax.numpy as jnp
import ml_dtypes
import numpy as np
from jax import lax
from jax.experimental import pallas as pl
from jax.experimental.pallas import tpu as pltpu
from jax.sharding import PartitionSpec as P


F32 = jnp.float32
BF16 = jnp.bfloat16
LANES = 128
GROUP = 16


def halves(table):
    high = table.astype(ml_dtypes.bfloat16)
    low = (table - high.astype(np.float64)).astype(ml_dtypes.bfloat16)
    return high, low


def transform_tables(tokens):
    rows = tokens // LANES
    length = 2 * tokens
    per_sender = rows // 64
    order = np.arange(rows).reshape(64 // GROUP, GROUP, per_sender)
    order = order.transpose(0, 2, 1).reshape(-1)
    k1 = np.arange(rows) + 0.5
    theta = 2.0 * np.pi * ((k1[:, None] * order[None, :]) % (2 * rows)) / (2 * rows)
    outer = np.concatenate([np.cos(theta), -np.sin(theta)], axis=0)
    q = np.arange(LANES)
    phi = 2.0 * np.pi * ((q[:, None] * q[None, :]) % LANES) / LANES
    c, s = np.cos(phi), np.sin(phi)
    inner = np.block([[c, -s], [s, c]])
    twist = 2.0 * np.pi * k1[:, None] * q[None, :] / length
    twiddle = np.stack([np.cos(twist), -np.sin(twist)]).astype(np.float32)
    scale = 2.0 / length
    return (
        np.concatenate(halves(outer), axis=0),
        np.concatenate(halves(inner) + halves(inner.T), axis=0),
        np.concatenate(halves(outer.T * scale), axis=0),
        twiddle,
    )


def exchange_table(rows):
    table = np.zeros((GROUP, rows, rows, GROUP), np.float32)
    for e in range(GROUP):
        for r in range(rows):
            table[e, r, r, e] = 1.0
    return table.reshape(GROUP * rows, rows * GROUP).astype(ml_dtypes.bfloat16)


def dot(left, right, dims=((1,), (0,))):
    return lax.dot_general(left, right, (dims, ((), ())), preferred_element_type=F32)


def split_up(value):
    high = value.astype(BF16)
    return high, (value - high.astype(F32)).astype(BF16)


def dot_left(table_high, table_low, value):
    value = value.astype(BF16)
    return dot(table_high, value) + dot(table_low, value)


def dot_right(value, table_high, table_low):
    value = value.astype(BF16)
    return dot(value, table_high) + dot(value, table_low)


def write_messages(out_ref, swap, blocks):
    size = swap.shape[0]
    for g, block in enumerate(blocks):
        rows = jnp.concatenate(block, axis=0)
        out_ref[g * size : (g + 1) * size, :] = dot(swap, rows).astype(BF16)


def read_messages(in_ref, swap):
    size = swap.shape[0]
    return [
        dot(swap, in_ref[g * size : (g + 1) * size, :], ((0,), (0,))).astype(BF16)
        for g in range(64 // GROUP)
    ]


def lane_blocks(value):
    return [value[:, u * LANES : (u + 1) * LANES] for u in range(value.shape[1] // LANES)]


def by_run(values):
    parts = [x for value in values for x in lane_blocks(value)]
    return [[x[g * GROUP : (g + 1) * GROUP] for x in parts] for g in range(64 // GROUP)]


def whole_signal(groups, k):
    return jnp.concatenate([x[k * 64 : (k + 1) * 64] for x in groups], axis=0)


def pack_kernel(in_ref, grad_ref, own_ref, sem):
    half = own_ref.shape[0] // 2
    copies = [
        pltpu.make_async_copy(in_ref, own_ref.at[pl.ds(0, half), :], sem),
        pltpu.make_async_copy(grad_ref, own_ref.at[pl.ds(half, half), :], sem),
    ]
    for copy in copies:
        copy.start()
    for copy in copies:
        copy.wait()


def fetch_kernel(*refs):
    *refs, sem = refs
    count = len(refs) // 2
    copies = [pltpu.make_async_copy(a, b, sem) for a, b in zip(refs[:count], refs[count:])]
    for copy in copies:
        copy.start()
    for copy in copies:
        copy.wait()


def project_kernel(
    ch_ref, own_ref, got1_ref, got3_ref, got2_ref, wv_ref, wg_ref, wo_ref, taps_ref, swap_ref,
    msg_ref, gate_ref, dgated_ref, in_ref, grad_ref,
):
    ch = ch_ref[0]
    for shift, ref in ((0, own_ref), (1, got1_ref), (3, got3_ref), (2, got2_ref)):
        at = pl.multiple_of((ch ^ shift) * 64, 64)
        in_ref[pl.ds(at, 64), :] = ref[:64, :]
        grad_ref[pl.ds(at, 64), :] = ref[64:, :]
    full_in = in_ref[...]
    value = dot(wv_ref[...], full_in).astype(BF16)
    gate = dot(wg_ref[...], full_in)
    d_gated = dot(wo_ref[...], grad_ref[...])
    gate_ref[...] = gate
    dgated_ref[...] = d_gated
    d_mixed = (d_gated * gate).astype(BF16)
    signals = (value, d_mixed, *split_up(taps_ref[...]))
    write_messages(msg_ref, swap_ref[...], by_run(signals))


def spectrum(first, tw_re, tw_im, table_high, table_low):
    half = first.shape[0] // 2
    re, im = first[:half], first[half:]
    z = jnp.concatenate([re * tw_re - im * tw_im, re * tw_im + im * tw_re], axis=1)
    return dot_right(z, table_high, table_low)


def convolve_kernel(
    got_ref, swap_ref, half_swap_ref, outer_ref, inner_ref, last_ref, tw_ref, out_ref, filt_ref
):
    rows = outer_ref.shape[0] // 2
    size = 2 * LANES
    ih, il, jh, jl = (inner_ref[k * size : (k + 1) * size, :] for k in range(4))
    groups = read_messages(got_ref, swap_ref[...])
    v, d, high, low = (whole_signal(groups, k) for k in range(4))
    first = dot(outer_ref[:rows, :], jnp.concatenate([v, d, high, low], axis=1))
    more = dot(outer_ref[rows:, :], jnp.concatenate([v, d, high], axis=1))
    tw_re, tw_im = tw_ref[0], tw_ref[1]
    firsts, mores = lane_blocks(first), lane_blocks(more)
    firsts = [firsts[0] + mores[0], firsts[1] + mores[1], firsts[2] + firsts[3] + mores[2]]
    v, d, h = (lane_blocks(spectrum(x, tw_re, tw_im, ih, il)) for x in firsts)
    (v_re, v_im), (d_re, d_im), (h_re, h_im) = v, d, h
    products = (
        (h_re * v_re - h_im * v_im, h_re * v_im + h_im * v_re),
        (h_re * d_re + h_im * d_im, h_re * d_im - h_im * d_re),
        (v_re * d_re + v_im * d_im, v_re * d_im - v_im * d_re),
    )
    back = []
    for re, im in products:
        y = dot_right(jnp.concatenate([re, im], axis=1), jh, jl)
        re, im = lane_blocks(y)
        b = jnp.concatenate([re * tw_re + im * tw_im, im * tw_re - re * tw_im], axis=0)
        back.append(dot_left(last_ref[: rows // 2, :], last_ref[rows // 2 :, :], b))
    mixed, d_value, d_filter = back
    swap = half_swap_ref[...]
    for ref, signals in (
        (out_ref, (mixed.astype(BF16), d_value.astype(BF16))),
        (filt_ref, split_up(d_filter)),
    ):
        blocks = [[x[g * 64 : (g + 1) * 64] for x in signals] for g in range(64 // GROUP)]
        write_messages(ref, swap, blocks)


def received_signal(groups, k):
    cols = []
    for u in range(4):
        at = (k * 4 + u) * GROUP
        cols.append(jnp.concatenate([x[at : at + GROUP] for x in groups], axis=0))
    return jnp.concatenate(cols, axis=1)


def gradient_kernel(
    ch_ref, got_ref, taps_ref, swap_ref, gate_ref, dgated_ref, in_ref, grad_ref, wv_ref, wg_ref,
    sums_ref, own_ref, send1_ref, send3_ref, send2_ref, part_ref
):
    groups = read_messages(got_ref, swap_ref[...])

    mixed = received_signal(groups, 0).astype(F32)
    d_value = received_signal(groups, 1)
    gated_out = (gate_ref[...] * mixed).astype(BF16)
    d_gate = (dgated_ref[...] * mixed).astype(BF16)
    both = jnp.concatenate([d_value, d_gate], axis=0)
    weights = jnp.concatenate([wv_ref[...], wg_ref[...]], axis=0)
    part_ref[...] = dot(weights, both, ((0,), (0,)))
    ch = ch_ref[0]

    def block(shift):
        at = pl.multiple_of((ch ^ shift) * 64, 64)
        return part_ref[pl.ds(at, 64), :]

    own_ref[...] = block(0)
    send1_ref[...] = block(1).astype(BF16)
    send3_ref[...] = block(3).astype(BF16)
    send2_ref[...] = block(2).astype(BF16)
    term = dot(both, in_ref[...], ((1,), (1,)))
    out_term = dot(gated_out, grad_ref[...], ((1,), (1,)))
    tiles = []
    for value in (term, out_term):
        for a in range(value.shape[0] // 8):
            tiles += lane_blocks(value[8 * a : 8 * a + 8])
    tiles += [jnp.zeros_like(tiles[0])] * (64 - len(tiles))
    taps = taps_ref[...].astype(F32)
    rows = [x for i, tile in enumerate(tiles) for x in (tile, taps[8 * i : 8 * i + 8])]
    sums_ref[...] = jnp.concatenate(rows, axis=0).astype(BF16)


def total_kernel(got_ref, out_ref, *, scale):
    got = got_ref[...].astype(F32).reshape(64, 16, LANES)
    total = got[:, :8].sum(axis=0) * scale
    whole = jnp.broadcast_to(total[None], (64, 8, LANES)).reshape(512, LANES)
    out_ref[...] = whole.astype(BF16)


def taps_kernel(got_ref, swap_ref, filt_ref, *, scale):
    groups = read_messages(got_ref, swap_ref[...])
    high, low = received_signal(groups, 2), received_signal(groups, 3)
    filt_ref[...] = (high.astype(F32) + low.astype(F32)) * scale


def settle_kernel(
    got_ref, own_ref, came1_ref, came3_ref, came2_ref, din_ref, dwv_ref, dwg_ref, dwo_ref
):
    d_inputs = own_ref[...]
    for ref in (came1_ref, came3_ref, came2_ref):
        d_inputs = d_inputs + ref[...].astype(F32)
    din_ref[...] = d_inputs.astype(BF16)
    for k, ref in enumerate((dwv_ref, dwg_ref, dwo_ref)):
        for a in range(8):
            at = 16 * (8 * k + a)
            pair = got_ref[at : at + 16, :].astype(F32)
            ref[8 * a : 8 * a + 8, :] = jnp.concatenate([pair[:8], pair[8:]], axis=1)


ANY = pl.BlockSpec(memory_space=pl.ANY)
VMEM = pl.BlockSpec(memory_space=pltpu.VMEM)
SMEM = pl.BlockSpec(memory_space=pltpu.SMEM)


def near(value):
    return pltpu.with_memory_space_constraint(value, pltpu.VMEM)


def far(value):
    return pltpu.with_memory_space_constraint(value, pltpu.HBM)


def call(kernel, outs, *args, scalar=None, scratch=()):
    many = isinstance(outs, list)
    specs = [VMEM] * len(args)
    args = [near(x) for x in args]
    if scalar is not None:
        specs, args = ([SMEM] + specs, [scalar] + args)
    return pl.pallas_call(
        kernel,
        out_shape=tuple(outs) if many else outs,
        in_specs=specs,
        out_specs=(VMEM,) * len(outs) if many else VMEM,
        scratch_shapes=scratch,
        compiler_params=pltpu.CompilerParams(vmem_limit_bytes=16 << 20),
    )(*args)


def copied(kernel, outs, *args):
    return pl.pallas_call(
        kernel,
        out_shape=tuple(outs),
        in_specs=[ANY] * len(args),
        out_specs=(VMEM,) * len(outs),
        scratch_shapes=[pltpu.SemaphoreType.DMA(())],
        compiler_params=pltpu.CompilerParams(vmem_limit_bytes=16 << 20),
    )(*[far(x) for x in args])


def exchanged(rows, axis):
    count = lax.axis_size(axis)
    parts = rows.reshape(count, rows.shape[0] // count, rows.shape[1])
    return lax.all_to_all(parts, axis, 0, 0, tiled=True).reshape(rows.shape)


def shifted(value, shift):
    return lax.ppermute(value, "ch", [(i, i ^ shift) for i in range(4)])


def on_device(inputs, w_value, w_gate, w_out, filter_taps, grad_out):
    tokens = filter_taps.shape[1] * lax.axis_size("seq")
    scale = 1.0 / math.sqrt(tokens)
    outer, inner, last, twiddle = [jnp.asarray(t) for t in transform_tables(tokens)]
    swap = jnp.asarray(exchange_table(16))
    half_swap = jnp.asarray(exchange_table(8))
    ch = lax.axis_index("ch").astype(jnp.int32).reshape(1)
    inside = pltpu.VMEM
    outside = jax.ShapeDtypeStruct

    rows, length = inputs.shape
    (own,) = copied(pack_kernel, [inside((2 * rows, length), inputs.dtype)], inputs, grad_out)
    later = (w_value.T, w_gate.T, w_out, filter_taps, twiddle)
    got = [shifted(own, s) for s in (1, 3)]
    got.append(shifted(own, 2))
    wv, wg, wo, taps, tw = copied(fetch_kernel, [inside(x.shape, x.dtype) for x in later], *later)
    msg, gate, d_gated, full_in, full_grad = call(
        project_kernel,
        [
            inside((1024, LANES), BF16),
            inside((64, 512), F32),
            inside((64, 512), F32),
            inside((256, 512), BF16),
            inside((256, 512), BF16),
        ],
        own, *got, wv, wg, wo, taps, swap, scalar=ch,
    )
    back, taps_back = call(
        convolve_kernel, [inside((512, LANES), BF16)] * 2,
        exchanged(msg, "seq"), swap, half_swap, outer, inner, last, tw,
    )
    sums, mine, send1, send3, send2 = call(
        gradient_kernel,
        [
            inside((1024, LANES), BF16),
            inside((64, 512), F32),
            inside((64, 512), BF16),
            inside((64, 512), BF16),
            inside((64, 512), BF16),
        ],
        exchanged(back, "seq"), taps_back, half_swap, gate, d_gated, full_in, full_grad, wv, wg,
        scalar=ch, scratch=[pltpu.VMEM((256, 512), F32)],
    )
    arrived = exchanged(sums, "seq")
    came3, came1 = shifted(send3, 3), shifted(send1, 1)
    total = call(
        lambda *refs: total_kernel(*refs, scale=scale),
        inside((512, LANES), BF16), arrived,
    )
    spread = exchanged(total, "seq")
    came2 = shifted(send2, 2)
    d_filter = call(
        lambda *refs: taps_kernel(*refs, scale=scale),
        outside((64, 512), F32), arrived, swap,
    )
    d_inputs, dwv, dwg, dwo = call(
        settle_kernel,
        [outside((64, 512), BF16)] + [outside((64, 256), F32)] * 3,
        spread, mine, came1, came3, came2,
    )
    return d_inputs, dwv.T, dwg.T, dwo, d_filter


def solution(mesh):
    placed = (
        P("ch", "seq"),
        P(None, "ch"),
        P(None, "ch"),
        P("ch", None),
        P("ch", "seq"),
        P("ch", "seq"),
    )
    return jax.shard_map(
        on_device,
        mesh=mesh,
        in_specs=placed,
        out_specs=(P("ch", "seq"), P(None, "ch"), P(None, "ch"), P("ch", None), P("ch", "seq")),
        check_vma=False,
    )
```
